256 devices in a mesh: grp: 8 (over y, x_lo), node: 32 (over x_hi, z, core).
Axes of the slice: x: 4 (x_hi: 2, x_lo: 2; x = x_hi * 2 + x_lo), y: 4, z: 8, core: 2. Of those that a mesh axis runs over, the one named last changes fastest.
Arguments:
- coefficients: float32 [65536, 1024], P(('grp', 'node')), may hold values from -6 to 6
- transfer: float32 [8, 65536, 512], P(None, ('grp', 'node')), may hold values from -0.3125 to 0.3125
- ranks: int32 [8, 256], P(None, ('grp', 'node')), may hold values from 128 to 256, as said below
Outputs:
- applied: float32 [65536, 1024], P(('grp', 'node'))
The draws below stay inside these ranges and needn't reach their ends.
Inputs may be any that keep to these rules, and one draw needn't show every extreme that they name: `ranks`: in each level some block has rank exactly 256 and some block rank 256 // 2.
All inputs are finite; a program needn't handle non-finite values.
Results may differ from the reference program's by a relative error of at most 0.00011.
Values sent between devices are 32-bit elements; how exact they have to be, the bound alone decides.
No kernel may reach another device: no remote copies, remote signals or barrier semaphores. Data moves between devices by JAX's collectives and lax.ppermute only.
A program may use at most 128 MiB of HBM per device.

```python
import jax
import jax.numpy as jnp
from jax import lax

K = 256
R = 1024
LEVELS = 8
BLOCKS = 256
ORDER = 65536
N_GRP = 8
N_NODE = 32


def draw_ranks(key, part):
    values = jax.random.randint(key, (LEVELS, BLOCKS), K // 2, K + 1).astype(jnp.int32)
    top_pos = jax.random.randint(jax.random.fold_in(key, 11), (LEVELS,), 0, BLOCKS)
    low_pos = (top_pos + 1 + jax.random.randint(jax.random.fold_in(key, 12), (LEVELS,), 0, BLOCKS - 1)) % BLOCKS
    level_ids = jnp.arange(LEVELS)
    values = values.at[level_ids, top_pos].set(K)
    values = values.at[level_ids, low_pos].set(K // 2)
    return values.astype(jnp.int32)


def block_scale(rng, dims, shards, least, top_value):
    def one(dim, parts):
        draws = jax.random.uniform(jax.random.fold_in(jax.random.fold_in(rng, 6), dim), (parts,), jnp.float32, least / len(shards), top_value / len(shards))
        return jnp.repeat(jnp.exp(draws), dims[dim] // parts).reshape((-1,) + (1,) * (len(dims) - dim - 1))

    level = one(*shards[0])
    for cut in shards[1:]:
        level = level * one(*cut)
    return level


def gaussian(key, dims, spread, bound, cuts=(), kind=jnp.bfloat16):
    drawn = spread * jax.random.normal(key, dims, jnp.float32)
    if cuts:
        drawn = drawn * block_scale(key, dims, cuts, -0.22, 0.18)
    return jnp.clip(drawn, -bound, bound).astype(kind)


def setup_inputs(seed: int = 0) -> dict:
    splits = jax.random.split(jax.random.key(seed), 4)
    return {
        "coefficients": gaussian(splits[0], (ORDER, R), 1.0, 6.0, ((0, 256),), jnp.float32),
        "transfer": gaussian(splits[1], (LEVELS, ORDER, 2 * K), (K * 3 // 2) ** -0.5, 0.3125, ((1, 256),), jnp.float32),
        "ranks": draw_ranks(jax.random.fold_in(splits[3], 71), 0),
    }


def reference(coefficients, transfer, ranks):
    blocks = N_GRP * N_NODE
    current = coefficients.reshape(blocks, K, R)
    row_ids = jnp.arange(K, dtype=jnp.int32)
    for level in range(LEVELS):
        span = 2 ** level
        outer = blocks // (2 * span)
        paired = current.reshape(outer, 2, span, K, R)
        stacked = jnp.concatenate([paired[:, 0], paired[:, 1]], axis=2)
        matrices = transfer[level].reshape(outer, 2, span, K, 2 * K)
        mixed = jnp.einsum("aibkm,abmr->aibkr", matrices, stacked, precision=lax.Precision.HIGHEST)
        limits = ranks[level].reshape(outer, 2, span)
        keep = row_ids[None, None, None, :] < limits[..., None]
        current = jnp.where(keep[..., None], mixed, jnp.zeros_like(mixed)).reshape(blocks, K, R)
    return current.reshape(blocks * K, R)
```

```python
import jax
import jax.numpy as jnp
from jax import lax
from jax.sharding import PartitionSpec as P

WIDTHS = (256, 256, 256, 256)
ORDER = ((0, 0), (0, 1), (1, 0), (0, 2), (1, 1), (2, 0), (0, 3), (1, 2), (2, 1), (3, 0), (0, 4), (1, 3), (2, 2), (3, 1), (0, 5), (1, 4), (2, 3), (3, 2), (0, 6), (1, 5), (2, 4), (3, 3), (0, 7), (1, 6), (2, 5), (3, 4), (1, 7), (2, 6), (3, 5), (2, 7), (3, 6), (3, 7))


def per_device(coefficients, transfer, ranks):
    node_bits = lax.axis_size("node").bit_length() - 1
    group_bits = lax.axis_size("grp").bit_length() - 1
    levels = node_bits + group_bits
    width = coefficients.shape[0]
    node_place, group_place = lax.axis_index("node"), lax.axis_index("grp")
    starts = [sum(WIDTHS[:i]) for i in range(len(WIDTHS))]

    def place(level):
        if level < node_bits:
            return "node", level, node_place >> level & 1
        return "grp", level - node_bits, group_place >> (level - node_bits) & 1

    def exchange(values, level):
        axis, bit, _ = place(level)
        return lax.ppermute(values, axis, [(i, i ^ 1 << bit) for i in range(lax.axis_size(axis))])

    def halves(matrices, limits, level):
        upper = place(level)[2]
        rows = lax.broadcasted_iota(jnp.int32, matrices.shape[1:], 0)
        matrix = jnp.where(rows < limits[level, 0], matrices[level], 0.0)
        return (
            lax.dynamic_slice_in_dim(matrix, upper * width, width, 1),
            lax.dynamic_slice_in_dim(matrix, (1 - upper) * width, width, 1),
        )

    def dot(a, b):
        return jnp.dot(a, b, precision=lax.Precision.HIGH, preferred_element_type=jnp.float32)

    def columns(values, chunk):
        return values[:, starts[chunk] : starts[chunk] + WIDTHS[chunk]]

    from_core = exchange(coefficients, 0)
    own, other = halves(transfer, ranks, 0)
    halved = {0: (own, other)}
    state, partner = {}, {}
    last = None
    for chunk, level in ORDER:
        if level == 0:
            mine, got = columns(coefficients, chunk), columns(from_core, chunk)
        else:
            mine, got = state[chunk], partner[chunk]
        if last is not None:
            mine, last = lax.optimization_barrier((mine, last))
        if level not in halved:
            halved[level] = halves(transfer, ranks, level)
        own, other = halved[level]
        first = dot(own, mine)
        if level:
            got, first = lax.optimization_barrier((got, first))
        state[chunk] = last = first + dot(other, got)
        if (chunk, level) == ORDER[0]:
            transfer, ranks, last = lax.optimization_barrier((transfer, ranks, last))
        if level + 1 < levels:
            partner[chunk] = exchange(state[chunk], level + 1)
    return jnp.concatenate([state[chunk] for chunk in range(len(WIDTHS))], axis=1)


def solution(mesh):
    return jax.shard_map(
        per_device,
        mesh=mesh,
        in_specs=(
            P(("grp", "node"), None),
            P(None, ("grp", "node"), None),
            P(None, ("grp", "node")),
        ),
        out_specs=P(("grp", "node"), None),
        check_vma=False,
    )
```

```python
import functools

import jax
import jax.numpy as jnp
from jax import lax
from jax.experimental import pallas as pl
from jax.experimental.pallas import tpu as pltpu
from jax.sharding import PartitionSpec as P

WIDTHS = (384, 256, 256, 128)
ORDER = ((0, 0), (0, 1), (1, 0), (0, 2), (1, 1), (2, 0), (1, 2), (0, 3), (3, 0), (2, 1), (0, 4), (1, 3), (3, 1), (2, 2), (1, 4), (0, 5), (1, 5), (2, 3), (3, 2), (0, 6), (2, 4), (1, 6), (3, 3), (0, 7), (2, 5), (3, 4), (3, 5), (1, 7), (2, 6), (3, 6), (2, 7), (3, 7))
VMEM = pl.BlockSpec(memory_space=pltpu.VMEM)
SMEM = pl.BlockSpec(memory_space=pltpu.SMEM)
COST = pl.CostEstimate(flops=2000000000, bytes_accessed=4000000, transcendentals=0)


def split(values):
    high = values.astype(jnp.bfloat16)
    return high, (values - high.astype(jnp.float32)).astype(jnp.bfloat16)


def prepare_kernel(first, device_ref, ranks_ref, matrix_ref, out_ref):
    step = pl.program_id(0)
    level = step + first
    width = out_ref.shape[1]
    upper = device_ref[0] >> level & 1
    rows = lax.broadcasted_iota(jnp.int32, (width, width), 0)
    keep = rows < ranks_ref[level, 0]
    for part in range(2):
        start = pl.multiple_of((upper ^ part) * width, width)
        half = jnp.where(keep, matrix_ref[0, :, pl.ds(start, width)], 0.0)
        high, low = split(half)
        for place, term in enumerate((high, high, low)):
            column = (3 * part + place) * width
            out_ref[step, :, column : column + width] = term


def prepare(device, ranks, transfer, first, count):
    _, width, both = transfer.shape
    return pl.pallas_call(
        functools.partial(prepare_kernel, first),
        grid=(count,),
        in_specs=[SMEM, SMEM, pl.BlockSpec((1, width, both), lambda i: (i + first, 0, 0))],
        out_specs=VMEM,
        out_shape=jax.ShapeDtypeStruct((count, width, 3 * both), jnp.bfloat16),
        compiler_params=pltpu.CompilerParams(vmem_limit_bytes=24 << 20),
        cost_estimate=COST,
        name="prepare",
    )(device, ranks, transfer)


def own_kernel(index, span, weights_ref, mine_ref, out_ref):
    high, low = split(mine_ref[:, span])
    terms = jnp.concatenate([high, low, high], axis=0)
    out_ref[...] = jnp.dot(
        weights_ref[index, :, : terms.shape[0]], terms, preferred_element_type=jnp.float32
    )


def other_kernel(index, span, weights_ref, own_ref, got_ref, out_ref):
    high, low = split(got_ref[:, span])
    terms = jnp.concatenate([high, low, high], axis=0)
    out_ref[...] = own_ref[...] + jnp.dot(
        weights_ref[index, :, terms.shape[0] :], terms, preferred_element_type=jnp.float32
    )


def mix(kernel, index, start, count, *operands):
    width = operands[-1].shape[0]
    return pl.pallas_call(
        functools.partial(kernel, index, slice(start, start + count)),
        in_specs=[VMEM] * len(operands),
        out_specs=VMEM,
        out_shape=jax.ShapeDtypeStruct((width, count), jnp.float32),
        compiler_params=pltpu.CompilerParams(vmem_limit_bytes=16 << 20),
        cost_estimate=COST,
        name="mix",
    )(*operands)


def per_device(coefficients, transfer, ranks):
    levels = transfer.shape[0]
    place = lax.axis_index(("grp", "node"))
    devices = lax.axis_size(("grp", "node"))
    device = place.astype(jnp.int32)[None]
    starts = [sum(WIDTHS[:i]) for i in range(len(WIDTHS))]

    def exchange(values, level):
        pairs = [(i, i ^ 1 << level) for i in range(devices)]
        return lax.ppermute(values, ("grp", "node"), pairs)

    from_core = exchange(coefficients, 0)
    weights = prepare(device, ranks, transfer, 0, 1)
    state, partner = {}, {}
    last = None
    for chunk, level in ORDER:
        if level == 0:
            matrix, index, mine, got = weights, 0, coefficients, from_core
            start = starts[chunk]
        else:
            matrix, index, mine, got = later, level - 1, state[chunk], partner[chunk]
            start = 0
        if last is not None:
            mine, last = lax.optimization_barrier((mine, last))
        total = mix(own_kernel, index, start, WIDTHS[chunk], matrix, mine)
        got, total = lax.optimization_barrier((got, total))
        total = mix(other_kernel, index, start, WIDTHS[chunk], matrix, total, got)
        state[chunk] = last = total
        if level + 1 < levels:
            partner[chunk] = exchange(state[chunk], level + 1)
        if (chunk, level) == ORDER[0]:
            held, last = lax.optimization_barrier((ranks, last))
            later = prepare(device, held, transfer, 1, levels - 1)
    return jnp.concatenate([state[chunk] for chunk in range(len(WIDTHS))], axis=1)


def solution(mesh):
    return jax.shard_map(
        per_device,
        mesh=mesh,
        in_specs=(
            P(("grp", "node"), None),
            P(None, ("grp", "node"), None),
            P(None, ("grp", "node")),
        ),
        out_specs=P(("grp", "node"), None),
        check_vma=False,
    )
```

```python
import functools

import jax
import jax.numpy as jnp
from jax import lax
from jax.experimental import pallas as pl
from jax.experimental.pallas import tpu as pltpu
from jax.sharding import PartitionSpec as P

WIDTHS = (384, 256, 256, 128)
ORDER = ((0, 0), (0, 1), (1, 0), (0, 2), (1, 1), (2, 0), (3, 0), (1, 2), (0, 3), (2, 1), (0, 4), (1, 3), (3, 1), (2, 2), (1, 4), (0, 5), (1, 5), (2, 3), (3, 2), (0, 6), (2, 4), (1, 6), (3, 3), (0, 7), (2, 5), (3, 4), (3, 5), (1, 7), (2, 6), (3, 6), (2, 7), (3, 7))
VMEM = pl.BlockSpec(memory_space=pltpu.VMEM)
SMEM = pl.BlockSpec(memory_space=pltpu.SMEM)
COST = pl.CostEstimate(flops=2000000000, bytes_accessed=4000000, transcendentals=0)


def split(values):
    high = values.astype(jnp.bfloat16)
    return high, (values - high.astype(jnp.float32)).astype(jnp.bfloat16)


def prepare_kernel(first, device_ref, ranks_ref, matrix_ref, out_ref):
    step = pl.program_id(0)
    level = step + first
    width = out_ref.shape[1]
    upper = device_ref[0] >> level & 1
    rows = lax.broadcasted_iota(jnp.int32, (width, width), 0)
    keep = rows < ranks_ref[0, level]
    for part in range(2):
        start = pl.multiple_of((upper ^ part) * width, width)
        half = jnp.where(keep, matrix_ref[0, :, pl.ds(start, width)], 0.0)
        high, low = split(half)
        for place, term in enumerate((high, high, low)):
            column = (3 * part + place) * width
            out_ref[step, :, column : column + width] = term


def prepare(device, ranks, transfer, first, count):
    _, width, both = transfer.shape
    return pl.pallas_call(
        functools.partial(prepare_kernel, first),
        grid=(count,),
        in_specs=[SMEM, SMEM, pl.BlockSpec((1, width, both), lambda i: (i + first, 0, 0))],
        out_specs=VMEM,
        out_shape=jax.ShapeDtypeStruct((count, width, 3 * both), jnp.bfloat16),
        compiler_params=pltpu.CompilerParams(vmem_limit_bytes=24 << 20),
        cost_estimate=COST,
        name="prepare",
    )(device, ranks, transfer)


def own_kernel(index, span, weights_ref, mine_ref, out_ref):
    high, low = split(mine_ref[:, span])
    terms = jnp.concatenate([high, low, high], axis=0)
    out_ref[...] = jnp.dot(
        weights_ref[index, :, : terms.shape[0]], terms, preferred_element_type=jnp.float32
    )


def other_kernel(index, span, weights_ref, own_ref, got_ref, out_ref):
    high, low = split(got_ref[:, span])
    terms = jnp.concatenate([high, low, high], axis=0)
    out_ref[...] = own_ref[...] + jnp.dot(
        weights_ref[index, :, terms.shape[0] :], terms, preferred_element_type=jnp.float32
    )


def mix(kernel, index, start, count, *operands):
    width = operands[-1].shape[0]
    return pl.pallas_call(
        functools.partial(kernel, index, slice(start, start + count)),
        in_specs=[VMEM] * len(operands),
        out_specs=VMEM,
        out_shape=jax.ShapeDtypeStruct((width, count), jnp.float32),
        compiler_params=pltpu.CompilerParams(vmem_limit_bytes=16 << 20),
        cost_estimate=COST,
        name="mix",
    )(*operands)


def per_device(coefficients, transfer, ranks):
    levels = transfer.shape[0]
    ranks = ranks.T
    place = lax.axis_index(("grp", "node"))
    devices = lax.axis_size(("grp", "node"))
    device = place.astype(jnp.int32)[None]
    starts = [sum(WIDTHS[:i]) for i in range(len(WIDTHS))]

    def exchange(values, level):
        pairs = [(i, i ^ 1 << level) for i in range(devices)]
        return lax.ppermute(values, ("grp", "node"), pairs)

    from_core = exchange(coefficients, 0)
    weights = prepare(device, ranks, transfer, 0, 1)
    state, partner = {}, {}
    last = None
    for chunk, level in ORDER:
        if level == 0:
            matrix, index, mine, got = weights, 0, coefficients, from_core
            start = starts[chunk]
        else:
            matrix, index, mine, got = later, level - 1, state[chunk], partner[chunk]
            start = 0
        if last is not None:
            mine, last = lax.optimization_barrier((mine, last))
        total = mix(own_kernel, index, start, WIDTHS[chunk], matrix, mine)
        got, total = lax.optimization_barrier((got, total))
        total = mix(other_kernel, index, start, WIDTHS[chunk], matrix, total, got)
        state[chunk] = last = total
        if level + 1 < levels:
            partner[chunk] = exchange(state[chunk], level + 1)
        if (chunk, level) == ORDER[0]:
            held, last = lax.optimization_barrier((ranks, last))
            later = prepare(device, held, transfer, 1, levels - 1)
    return jnp.concatenate([state[chunk] for chunk in range(len(WIDTHS))], axis=1)


def solution(mesh):
    return jax.shard_map(
        per_device,
        mesh=mesh,
        in_specs=(
            P(("grp", "node"), None),
            P(None, ("grp", "node"), None),
            P(None, ("grp", "node")),
        ),
        out_specs=P(("grp", "node"), None),
        check_vma=False,
    )
```
